32 devices in a mesh: base: 16 (over z, x, core), chan: 2 (over y).
Axes of the slice: x: 2, y: 2, z: 4, core: 2. Of those that a mesh axis runs over, the one named last changes fastest.
Arguments:
- image0: float32 [2048, 2048], P(('base', 'chan')), may hold values from -6 to 6
- interp: float32 [16, 2, 256, 8, 256], P('base', 'chan'), may hold values from -0.375 to 0.375
- vis_weight: float32 [16, 2, 256, 8], P('base', 'chan'), may hold values from 0.2 to 5
- counts: int32 [16, 2, 256], P('base', 'chan'), may hold values from 1 to 8
- tile_index: int32 [16, 2, 256], P('base', 'chan'), may hold values from 0 to 511
Outputs:
- image_out: float32 [2048, 2048], P(('base', 'chan'))
- estimates: float32 [3], replicated
The draws below stay inside these ranges and needn't reach their ends.
Inputs may be any that keep to these rules, and one draw needn't show every extreme that they name: `tile_index`: slot s of a device belongs to the spectrum block of device s // 8 of base+chan, base index major; the entry numbers the tile within that block. `counts`: visibility v of a slot is live when v < count.
All inputs are finite; a program needn't handle non-finite values.
Results may differ from the reference program's by a relative error of at most 0.00023.
Values sent between devices are 32-bit elements; how exact they have to be, the bound alone decides.
A program may use at most 128 MiB of HBM per device.

```python
import math
import jax
import jax.numpy as jnp
from jax import lax

N = 2048
TILE_V = 8
TILE_U = 32
VCAP = 8
TOUCH = 256
ITERS = 3
CAP = 8
TILES_OWN = 512
N_BASE = 16
N_CHAN = 2


def place_ends(values, stream_key, smallest, top_value):
    longest = values.shape.index(max(values.shape))
    spots = []
    for shift in (0, 1):
        where = [jax.random.randint(jax.random.fold_in(stream_key, axis), (), 0, length) for axis, length in enumerate(values.shape)]
        where[longest] = (where[longest] + shift) % values.shape[longest]
        spots.append(tuple(where))
    return values.at[spots[0]].set(smallest).at[spots[1]].set(top_value)


def shard_levels(stream_key, dims, shards, smallest, top_value):
    gain, own = 1.0, jax.random.fold_in(stream_key, 6)
    for dim, parts in shards:
        heights = jnp.exp(jax.random.uniform(jax.random.fold_in(own, dim), (parts,), jnp.float32, smallest / len(shards), top_value / len(shards)))
        gain = gain * jnp.repeat(heights, dims[dim] // parts).reshape([-1 if axis == dim else 1 for axis in range(len(dims))])
    return gain


def scatter_about(stream_key, extent, spread, most, cuts=(), kind=jnp.bfloat16):
    values = jax.random.normal(stream_key, extent, jnp.float32) * spread
    if len(cuts) > 0:
        values = shard_levels(stream_key, extent, cuts, -0.22, 0.18) * values
    return jnp.clip(values, min=-most, max=most).astype(kind)


def setup_inputs(seed: int = 0) -> dict:
    splits = jax.random.split(jax.random.key(seed), 6)
    image0 = scatter_about(splits[0], (N, N), 1.0, 6.0, ((0, 32),), jnp.float32)
    interp = scatter_about(splits[1], (N_BASE, N_CHAN, TOUCH, VCAP, TILE_V * TILE_U), (TILE_V * TILE_U) ** -0.5, 0.375, ((0, 16), (1, 2)), jnp.float32)
    vis_weight = jnp.clip(jnp.exp(math.log(5.0) - 3.218876 * jax.random.uniform(splits[2], (N_BASE, N_CHAN, TOUCH, VCAP), jnp.float32) ** shard_levels(splits[2], (N_BASE, N_CHAN, TOUCH, VCAP), ((0, 16), (1, 2)), -0.2, 0.2)), 0.2, 5.0)
    counts = place_ends(jax.random.randint(splits[3], (N_BASE, N_CHAN, TOUCH), 1, VCAP + 1), jax.random.fold_in(splits[3], 1), 1, VCAP).astype(jnp.int32)
    tile_index = place_ends(jax.random.randint(splits[4], (N_BASE, N_CHAN, TOUCH), 0, TILES_OWN), jax.random.fold_in(splits[4], 1), 0, TILES_OWN - 1).astype(jnp.int32)
    return {"image0": image0, "interp": interp, "vis_weight": vis_weight, "counts": counts, "tile_index": tile_index}


PRECISION_LEVEL = lax.Precision.HIGHEST

def spectrum_tiles(image):
    devices = N_BASE * N_CHAN
    spectrum = jnp.fft.fft2(image, norm='ortho')
    planes = []
    for plane in (jnp.real(spectrum), jnp.imag(spectrum)):
        held = plane.T.reshape(devices, N // devices // TILE_V, TILE_V, N // TILE_U, TILE_U)
        planes.append(held.transpose(0, 1, 3, 2, 4).reshape(devices * TILES_OWN, TILE_V * TILE_U))
    return jnp.stack(planes, axis=1)

def image_of(grid):
    devices = N_BASE * N_CHAN
    planes = []
    for member in range(2):
        held = grid[:, member, :].reshape(devices, N // devices // TILE_V, N // TILE_U, TILE_V, TILE_U)
        planes.append(held.transpose(0, 1, 3, 2, 4).reshape(N, N).T)
    spectrum = lax.complex(planes[0], planes[1])
    return jnp.real(jnp.fft.ifft2(spectrum, norm='ortho'))

def apply_normal(image, sample_weights, masked_weight, global_index):
    tiles = spectrum_tiles(image)

    def accumulate(grid, pieces):
        slot_weight_table, slot_valid_mask, slot_index = pieces
        sample_values = tiles[slot_index]
        visible_samples = jnp.einsum('gnz,gez->gen', slot_weight_table, sample_values, precision=PRECISION_LEVEL) * slot_valid_mask[:, None, :]
        gridded_plane = jnp.einsum('hbi,hyb->hyi', slot_weight_table, visible_samples, precision=PRECISION_LEVEL)
        return (grid.at[slot_index].add(gridded_plane), None)
    grid, unused = lax.scan(accumulate, jnp.zeros_like(tiles), (sample_weights, masked_weight, global_index))
    return image_of(grid)

def reference(image0, interp, vis_weight, counts, tile_index):
    devices = N_BASE * N_CHAN
    sample_weights = interp.reshape(devices, TOUCH, VCAP, TILE_V * TILE_U)
    live = (jnp.arange(VCAP, dtype=jnp.int32)[None, None, :] < counts.reshape(devices, TOUCH, 1)).astype(jnp.float32)
    masked_weight = vis_weight.reshape(devices, TOUCH, VCAP) * live
    owner = (jnp.arange(TOUCH, dtype=jnp.int32) // CAP).astype(jnp.int32)
    global_index = (owner[None, :] * TILES_OWN + tile_index.reshape(devices, TOUCH)).astype(jnp.int32)
    current = image0 / jnp.sqrt(jnp.sum(image0 * image0))
    found = []
    for iteration in range(ITERS):
        image = apply_normal(current, sample_weights, masked_weight, global_index)
        norm_value = jnp.sqrt(jnp.sum(image * image))
        found.append(norm_value)
        current = image / norm_value
    return (N * current, jnp.stack(found))
```

```python
import math

import jax
import jax.numpy as jnp
import numpy as np
from jax import lax
from jax.experimental import pallas as pl
from jax.experimental.pallas import tpu as pltpu
from jax.sharding import PartitionSpec as P

TILE_V = 8
TILE_U = 32
ITERS = 3


PRECISION_LEVEL = lax.Precision.HIGHEST


def split_length(length):
    outer_len = 2 ** ((length.bit_length() - 1) // 2)
    return (outer_len, length // outer_len)


def angle_table(count_a, count_b, modulus, sign):
    left = jnp.arange(count_a, dtype=jnp.int32)[:, None]
    right = jnp.arange(count_b, dtype=jnp.int32)[None, :]
    angle = sign * 2.0 * math.pi / modulus * (left * right % modulus).astype(jnp.float32)
    return (jnp.cos(angle), jnp.sin(angle))


def transform_rows(real_part, imag_part, sign):
    row_count, length = real_part.shape
    outer_len, inner_len = split_length(length)
    cos_q, sin_q = angle_table(inner_len, inner_len, inner_len, sign)
    cos_t, sin_t = angle_table(inner_len, outer_len, length, sign)
    cos_p, sin_p = angle_table(outer_len, outer_len, outer_len, sign)
    real_in = real_part.reshape(row_count, inner_len, outer_len)
    first_re = jnp.einsum("kq,rqp->rkp", cos_q, real_in, precision=PRECISION_LEVEL)
    first_im = jnp.einsum("kq,rqp->rkp", sin_q, real_in, precision=PRECISION_LEVEL)
    if imag_part is not None:
        imag_in = imag_part.reshape(row_count, inner_len, outer_len)
        first_re = first_re - jnp.einsum("kq,rqp->rkp", sin_q, imag_in, precision=PRECISION_LEVEL)
        first_im = first_im + jnp.einsum("kq,rqp->rkp", cos_q, imag_in, precision=PRECISION_LEVEL)
    turned_re = first_re * cos_t - first_im * sin_t
    turned_im = first_re * sin_t + first_im * cos_t
    last_re = jnp.einsum("jp,rkp->rjk", cos_p, turned_re, precision=PRECISION_LEVEL) - jnp.einsum(
        "jp,rkp->rjk", sin_p, turned_im, precision=PRECISION_LEVEL
    )
    last_im = jnp.einsum("jp,rkp->rjk", cos_p, turned_im, precision=PRECISION_LEVEL) + jnp.einsum(
        "jp,rkp->rjk", sin_p, turned_re, precision=PRECISION_LEVEL
    )
    factor = 1.0 / math.sqrt(length)
    return (
        last_re.reshape(row_count, length) * factor,
        last_im.reshape(row_count, length) * factor,
    )


def transpose_global(real_part, imag_part):
    row_count, length = real_part.shape
    n_base = lax.axis_size("base")
    n_chan = lax.axis_size("chan")
    width = length // (n_base * n_chan)
    moved = (
        lax.all_to_all(
            lax.all_to_all(
                real_part.reshape(1, row_count, n_base, n_chan, width),
                "base",
                split_axis=2,
                concat_axis=0,
                tiled=True,
            ),
            "chan",
            split_axis=3,
            concat_axis=1,
            tiled=True,
        ),
        lax.all_to_all(
            lax.all_to_all(
                imag_part.reshape(1, row_count, n_base, n_chan, width),
                "base",
                split_axis=2,
                concat_axis=0,
                tiled=True,
            ),
            "chan",
            split_axis=3,
            concat_axis=1,
            tiled=True,
        ),
    )
    return (moved[0].reshape(length, width).T, moved[1].reshape(length, width).T)


def to_tiles(plane):
    row_count, length = plane.shape
    shaped = plane.reshape(row_count // TILE_V, TILE_V, length // TILE_U, TILE_U)
    return shaped.transpose(0, 2, 1, 3).reshape(-1, TILE_V * TILE_U)


def from_tiles(tiles, row_count, length):
    shaped = tiles.reshape(row_count // TILE_V, length // TILE_U, TILE_V, TILE_U)
    return shaped.transpose(0, 2, 1, 3).reshape(row_count, length)


def slot_work(sample_weights, masked_weight, sample_values):
    visible_samples = (
        jnp.einsum("gnz,gez->gen", sample_weights, sample_values, precision=PRECISION_LEVEL)
        * masked_weight[:, None, :]
    )
    return jnp.einsum("hbi,hyb->hyi", sample_weights, visible_samples, precision=PRECISION_LEVEL)


def total_squares(image):
    return lax.psum(jnp.sum(image * image), ("base", "chan"))


def general_device(image0, interp, vis_weight, counts, tile_index):
    n_base = lax.axis_size("base")
    n_chan = lax.axis_size("chan")
    row_count, length = image0.shape
    touch = tile_index.shape[2]
    slots_each = touch // (n_base * n_chan)
    vcap = interp.shape[3]
    cells = interp.shape[4]
    tiles_own = row_count // TILE_V * (length // TILE_U)
    live = (jnp.arange(vcap, dtype=jnp.int32)[None, :] < counts.reshape(touch, 1)).astype(
        jnp.float32
    )
    masked_weight = vis_weight.reshape(touch, vcap) * live
    sample_weights = interp.reshape(touch, vcap, cells)
    wanted = lax.all_to_all(
        lax.all_to_all(
            tile_index.reshape(n_base, n_chan, slots_each),
            "base",
            split_axis=0,
            concat_axis=0,
            tiled=True,
        ),
        "chan",
        split_axis=1,
        concat_axis=1,
        tiled=True,
    ).reshape(touch)
    onehot = (jnp.arange(tiles_own, dtype=jnp.int32)[:, None] == wanted[None, :]).astype(
        jnp.float32
    )
    moved = (
        lax.all_to_all(
            lax.all_to_all(
                sample_weights.reshape(n_base, n_chan, slots_each, vcap, cells),
                "base",
                split_axis=0,
                concat_axis=0,
                tiled=True,
            ),
            "chan",
            split_axis=1,
            concat_axis=1,
            tiled=True,
        ),
        lax.all_to_all(
            lax.all_to_all(
                masked_weight.reshape(n_base, n_chan, slots_each, vcap),
                "base",
                split_axis=0,
                concat_axis=0,
                tiled=True,
            ),
            "chan",
            split_axis=1,
            concat_axis=1,
            tiled=True,
        ),
    )
    sample_weights = moved[0].reshape(touch, vcap, cells)
    masked_weight = moved[1].reshape(touch, vcap)
    found = []
    current = image0 / jnp.sqrt(total_squares(image0))
    for iteration in range(ITERS):
        real_part, imag_part = transform_rows(current, None, -1.0)
        real_part, imag_part = transpose_global(real_part, imag_part)
        real_part, imag_part = transform_rows(real_part, imag_part, -1.0)
        tiles = jnp.stack([to_tiles(real_part), to_tiles(imag_part)], axis=1)
        sample_values = jnp.take(tiles, wanted, axis=0)
        gridded_plane = slot_work(sample_weights, masked_weight, sample_values)
        summed = jnp.einsum("ts,skc->tkc", onehot, gridded_plane, precision=PRECISION_LEVEL)
        real_part = from_tiles(summed[:, 0, :], row_count, length)
        imag_part = from_tiles(summed[:, 1, :], row_count, length)
        real_part, imag_part = transform_rows(real_part, imag_part, 1.0)
        real_part, imag_part = transpose_global(real_part, imag_part)
        real_part, imag_part = transform_rows(real_part, imag_part, 1.0)
        norm_value = jnp.sqrt(total_squares(real_part))
        found.append(norm_value)
        current = real_part / norm_value
    return (float(length) * current, jnp.stack(found))


F32 = jnp.float32
BF16 = jnp.bfloat16
VMEM_SPEC = pl.BlockSpec(memory_space=pltpu.VMEM)
SMEM_SPEC = pl.BlockSpec(memory_space=pltpu.SMEM)
BIG = pltpu.CompilerParams(vmem_limit_bytes=48 * 1024 * 1024)


def halves(value):
    high = value.astype(BF16)
    return high, (value - high.astype(F32)).astype(BF16)


def np_halves(table):
    high = np.asarray(table, np.float32).astype(jnp.bfloat16)
    low = (np.asarray(table, np.float64) - high.astype(np.float64)).astype(jnp.bfloat16)
    return high, low


def triple_dot(left, right, dims):
    def one(a, b):
        return lax.dot_general(a, b, (dims, ((), ())), preferred_element_type=F32)

    return one(left[0], right[0]) + (one(left[0], right[1]) + one(left[1], right[0]))


def fft_list(items, sign):
    count = len(items)
    if count == 1:
        return items
    even = fft_list(items[0::2], sign)
    odd = fft_list(items[1::2], sign)
    low, high = [], []
    for k in range(count // 2):
        re, im = odd[k]
        if k == 0:
            t_re, t_im = re, im
        elif 4 * k == count:
            t_re, t_im = (im, -re) if sign < 0 else (-im, re)
        else:
            angle = sign * 2.0 * math.pi * k / count
            c, s = math.cos(angle), math.sin(angle)
            t_re, t_im = re * c - im * s, re * s + im * c
        e_re, e_im = even[k]
        low.append((e_re + t_re, e_im + t_im))
        high.append((e_re - t_re, e_im - t_im))
    return low + high


def exchange_kernel(n, n_chan, src_ref, dst_ref, own_sem, send_sem, recv_sem):
    me = lax.axis_index("base") * n_chan + lax.axis_index("chan")
    own = pltpu.make_async_copy(src_ref.at[me], dst_ref.at[me], own_sem)
    own.start()

    def copy(step):
        peer = lax.rem(me + step, n)
        return pltpu.make_async_remote_copy(
            src_ref=src_ref.at[peer],
            dst_ref=dst_ref.at[me],
            send_sem=send_sem.at[step],
            recv_sem=recv_sem.at[step],
            device_id=(peer // n_chan, lax.rem(peer, n_chan)),
            device_id_type=pl.DeviceIdType.MESH,
        )

    def launch(step, carry):
        copy(step).start()
        return carry

    def finish(step, carry):
        copy(step).wait()
        return carry

    lax.fori_loop(1, n, launch, 0)
    own.wait()
    lax.fori_loop(1, n, finish, 0)


def exchange(values, n, n_chan):
    return pl.pallas_call(
        lambda *refs: exchange_kernel(n, n_chan, *refs),
        out_shape=jax.ShapeDtypeStruct(values.shape, values.dtype),
        in_specs=[pl.BlockSpec(memory_space=pltpu.VMEM)],
        out_specs=pl.BlockSpec(memory_space=pltpu.VMEM),
        scratch_shapes=[
            pltpu.SemaphoreType.DMA,
            pltpu.SemaphoreType.DMA((n,)),
            pltpu.SemaphoreType.DMA((n,)),
        ],
        compiler_params=pltpu.CompilerParams(
            has_side_effects=True, vmem_limit_bytes=48 * 1024 * 1024
        ),
    )(values)


def turn(re, im, c, s):
    return re * c - im * s, re * s + im * c


def swap_halves(x0, x1):
    half = x0.shape[1] // 2
    left = lax.broadcasted_iota(jnp.int32, x0.shape, 1) < half
    return (
        jnp.where(left, x0, pltpu.roll(x1, half, 1)),
        jnp.where(left, pltpu.roll(x0, half, 1), x1),
    )


def row_inverse(n, recv_ref, tc_ref, ts_ref, mh_ref, ml_ref, b_ref):
    rows = recv_ref.shape[1] // 2

    def chunk(i, carry):
        at = pl.multiple_of(i * 8, 8)
        items = [
            (recv_ref[o, pl.ds(at, 8), :], recv_ref[o, pl.ds(at + rows, 8), :]) for o in range(n)
        ]
        items = fft_list(items, 1.0)
        items = [
            turn(*items[q], tc_ref[q, pl.ds(at, 8), :], -ts_ref[q, pl.ds(at, 8), :])
            for q in range(n)
        ]
        for pair in range(n // 2):
            for part in range(2):
                x0, x1 = swap_halves(items[2 * pair][part], items[2 * pair + 1][part])
                lanes = slice(pair * 128, (pair + 1) * 128)
                b_ref[pl.ds(at + part * 2 * rows, 8), lanes] = x0
                b_ref[pl.ds(at + part * 2 * rows + rows, 8), lanes] = x1
        return carry

    lax.fori_loop(0, rows // 8, chunk, 0)
    parts = []
    for start in range(0, b_ref.shape[1], 512):
        right = halves(b_ref[:, start : start + 512])
        parts.append(triple_dot((mh_ref[...], ml_ref[...]), right, ((1,), (0,))))
    return parts


def row_forward(n, parts, tc_ref, ts_ref, mh_ref, ml_ref, b_ref, send_ref):
    rows = tc_ref.shape[1]
    total = sum(jnp.sum(part * part) for part in parts)
    for index, part in enumerate(parts):
        b_ref[:, index * 512 : (index + 1) * 512] = triple_dot(
            (mh_ref[...], ml_ref[...]), halves(part), ((1,), (0,))
        )

    def chunk(i, carry):
        at = pl.multiple_of(i * 8, 8)
        items = [[None, None] for _ in range(n)]
        for pair in range(n // 2):
            for part in range(2):
                lanes = slice(pair * 128, (pair + 1) * 128)
                x0 = b_ref[pl.ds(at + part * 2 * rows, 8), lanes]
                x1 = b_ref[pl.ds(at + part * 2 * rows + rows, 8), lanes]
                items[2 * pair][part], items[2 * pair + 1][part] = swap_halves(x0, x1)
        items = [
            turn(*items[q], tc_ref[q, pl.ds(at, 8), :], ts_ref[q, pl.ds(at, 8), :])
            for q in range(n)
        ]
        items = fft_list(items, -1.0)
        for o in range(n):
            send_ref[o, pl.ds(at, 8), :] = items[o][0]
            send_ref[o, pl.ds(at + rows, 8), :] = items[o][1]
        return carry

    lax.fori_loop(0, rows // 8, chunk, 0)
    for o in range(n):
        send_ref[o, 2 * rows : 2 * rows + 8, :] = jnp.full((8, 128), total, F32)


def first_kernel(n, y_ref, tc, ts, fh, fl, send_ref, b_ref):
    parts = [y_ref[:, s : s + 512] for s in range(0, y_ref.shape[1], 512)]
    row_forward(n, parts, tc, ts, fh, fl, b_ref, send_ref)


def middle_kernel(n, recv_ref, tc, ts, fh, fl, ih, il, send_ref, b_ref):
    parts = row_inverse(n, recv_ref, tc, ts, ih, il, b_ref)
    row_forward(n, parts, tc, ts, fh, fl, b_ref, send_ref)


def last_kernel(n, recv_ref, tc, ts, ih, il, y_ref, sum_ref, b_ref):
    parts = row_inverse(n, recv_ref, tc, ts, ih, il, b_ref)
    for index, part in enumerate(parts):
        y_ref[:, index * 512 : (index + 1) * 512] = part
    total = sum(jnp.sum(part * part) for part in parts)
    for o in range(n):
        sum_ref[o] = jnp.full((8, 128), total, F32)


def column_kernel(
    n,
    tile_ref,
    recv_ref,
    wh_ref,
    wl_ref,
    wm_ref,
    tc,
    ts,
    fh,
    fl,
    ih,
    il,
    send_ref,
    norm_ref,
    u_ref,
    t_ref,
    acc_ref,
    g_ref,
):
    rows = send_ref.shape[1] // 2
    blocks = rows // 8
    groups = wh_ref.shape[0]
    members = g_ref.shape[0] // 2
    across = 2 * rows
    total = recv_ref[0, 2 * rows : 2 * rows + 8, :]
    for d in range(1, n):
        total = total + recv_ref[d, 2 * rows : 2 * rows + 8, :]
    norm = jnp.sqrt(total)
    norm_ref[...] = norm

    def forward(i, carry):
        at = pl.multiple_of(i * 8, 8)
        inverse = 1.0 / norm_ref[...]
        items = fft_list(
            [
                (
                    recv_ref[d, pl.ds(at, 8), :] * inverse,
                    recv_ref[d, pl.ds(at + rows, 8), :] * inverse,
                )
                for d in range(n)
            ],
            -1.0,
        )
        for k in range(n):
            re, im = turn(*items[k], tc[k : k + 1, :], ts[k : k + 1, :])
            u_ref[i, k * 8 : k * 8 + 8, :128] = re
            u_ref[i, k * 8 : k * 8 + 8, 128:] = im
        right = halves(u_ref[i])
        t_ref[i] = triple_dot((fh[...], fl[...]), right, ((1,), (1,)))
        acc_ref[i] = jnp.zeros(acc_ref.shape[1:], F32)
        return carry

    lax.fori_loop(0, blocks, forward, 0)

    row_of = lax.broadcasted_iota(jnp.int32, (2 * members, 256), 0) % members
    slot_of = lax.broadcasted_iota(jnp.int32, (2 * members, 256), 1) // (256 // members)

    def place(index):
        tile = tile_ref[index]
        column = tile // across
        row = (column // blocks) * across + tile % across
        return column % blocks, row

    def group(g, carry):
        for s in range(members):
            block, row = place(g * members + s)
            g_ref[s : s + 1, :] = t_ref[block, pl.ds(row, 1), :]
            g_ref[s + members : s + members + 1, :] = t_ref[block, pl.ds(row + 128, 1), :]
        weights = (wh_ref[g], wl_ref[g])
        seen = triple_dot(halves(g_ref[...]), weights, ((1,), (1,)))
        seen = jnp.where(row_of == slot_of, seen * wm_ref[g], 0.0)
        g_ref[...] = triple_dot(halves(seen), weights, ((1,), (0,)))
        for s in range(members):
            block, row = place(g * members + s)
            acc_ref[block, pl.ds(row, 1), :] += g_ref[s : s + 1, :]
            acc_ref[block, pl.ds(row + 128, 1), :] += g_ref[s + members : s + members + 1, :]
        return carry

    lax.fori_loop(0, groups, group, 0)

    def backward(i, carry):
        at = pl.multiple_of(i * 8, 8)
        u_ref[i] = triple_dot(halves(acc_ref[i].T), (ih[...], il[...]), ((1,), (0,)))
        items = []
        for k in range(n):
            re = u_ref[i, k * 8 : k * 8 + 8, :128]
            im = u_ref[i, k * 8 : k * 8 + 8, 128:]
            items.append(turn(re, im, tc[k : k + 1, :], -ts[k : k + 1, :]))
        items = fft_list(items, 1.0)
        for d in range(n):
            send_ref[d, pl.ds(at, 8), :] = items[d][0]
            send_ref[d, pl.ds(at + rows, 8), :] = items[d][1]
        return carry

    lax.fori_loop(0, blocks, backward, 0)


def weight_kernel(x_ref, perm_ref, high_ref, low_ref):
    count, _, cells = x_ref.shape
    value = x_ref[:, :64, :].reshape(count * 64, cells)
    for part, ref in zip(halves(value), (high_ref, low_ref)):
        ref[0] = jnp.dot(part, perm_ref[...], preferred_element_type=F32).astype(BF16)


def tables(n, row_count, length):
    half = row_count // 2
    scale = 1.0 / math.sqrt(length)
    local = np.arange(row_count)
    angle = -2.0 * np.pi * np.outer(local, local) / row_count
    c, s = np.cos(angle) * scale, np.sin(angle) * scale
    two = np.eye(2)
    col_f = np.block([[np.kron(two, c), np.kron(two, -s)], [np.kron(two, s), np.kron(two, c)]])
    col_i = np.block([[np.kron(two, c), np.kron(two, -s)], [np.kron(two, s), np.kron(two, c)]])
    row_f = np.concatenate([c, s], axis=0)
    row_i = np.concatenate([c, s], axis=1)
    index = np.arange(n)
    turns = -2.0 * np.pi * np.outer(index, np.tile(local, 2)) / length
    u = np.arange(half)[:, None] + half * (np.arange(2 * row_count)[None, :] // row_count)
    row_turns = -2.0 * np.pi * index[:, None, None] * u[None] / length
    return col_f, col_i, row_f, row_i, turns, row_turns


def fast_device(image0, interp, vis_weight, counts, tile_index):
    n_chan = lax.axis_size("chan")
    n = lax.axis_size("base") * n_chan
    row_count, length = image0.shape
    touch = tile_index.shape[2]
    each = touch // n
    vcap, cells = interp.shape[3:]
    members = cells // vcap
    groups = touch // members
    col_f, col_i, row_f, row_i, turns, row_turns = tables(n, row_count, length)
    cfh, cfl = np_halves(col_f)
    cih, cil = np_halves(col_i)
    rfh, rfl = np_halves(row_f)
    rih, ril = np_halves(row_i)
    tc, ts = np.cos(turns).astype(np.float32), np.sin(turns).astype(np.float32)
    rtc = np.cos(row_turns).astype(np.float32)
    rts = np.sin(row_turns).astype(np.float32)
    order = np.arange(cells).reshape(TILE_V, TILE_U).T.reshape(-1)
    perm = np.zeros((cells, cells), np.float32)
    perm[order, np.arange(cells)] = 1.0

    live = (jnp.arange(vcap, dtype=jnp.int32)[None, :] < counts.reshape(touch, 1)).astype(F32)
    masked = (vis_weight.reshape(touch, vcap) * live).reshape(n, 1, each * vcap)
    masked = jnp.pad(masked, ((0, 0), (0, 0), (0, cells - each * vcap)))
    numbers = tile_index.reshape(n, 1, each).astype(F32)
    numbers = jnp.pad(numbers, ((0, 0), (0, 6), (0, cells - each)))
    packed = jnp.concatenate([interp.reshape(n, each * vcap, cells), masked, numbers], axis=1)
    packed = jnp.pad(packed, ((0, 0), (0, 72 - packed.shape[1]), (0, 0)))
    packed = exchange(packed, n, n_chan)
    weights = packed[:, each * vcap, : each * vcap].reshape(groups, 1, members * vcap)
    wanted = packed[:, each * vcap + 1, :each].astype(jnp.int32).reshape(touch)
    span = n // groups
    wh, wl = pl.pallas_call(
        weight_kernel,
        grid=(groups,),
        out_shape=[jax.ShapeDtypeStruct((groups, members * vcap, cells), BF16)] * 2,
        in_specs=[
            pl.BlockSpec((span, 72, cells), lambda g: (g, 0, 0)),
            pl.BlockSpec((cells, cells), lambda g: (0, 0)),
        ],
        out_specs=[pl.BlockSpec((1, members * vcap, cells), lambda g: (g, 0, 0))] * 2,
    )(packed, jnp.asarray(perm, BF16))

    ready = jax.ShapeDtypeStruct((n, row_count + 8, 2 * row_count), F32)
    wide = [pltpu.VMEM((2 * row_count, length), F32)]

    def call(kernel, shapes, scratch, specs):
        return pl.pallas_call(
            lambda *refs: kernel(n, *refs),
            out_shape=shapes,
            in_specs=specs,
            out_specs=jax.tree.map(lambda _: VMEM_SPEC, shapes),
            scratch_shapes=scratch,
            compiler_params=BIG,
        )

    column = call(
        column_kernel,
        [
            jax.ShapeDtypeStruct((n, row_count, 2 * row_count), F32),
            jax.ShapeDtypeStruct((8, 128), F32),
        ],
        [pltpu.VMEM((row_count // 16, 256, 256), F32)] * 3 + [pltpu.VMEM((2 * members, cells), F32)],
        [SMEM_SPEC] + [VMEM_SPEC] * 10,
    )
    held = image0.reshape(row_count, length // n, n).transpose(1, 2, 0).reshape(length // n, -1)
    send = call(first_kernel, ready, wide, [VMEM_SPEC] * 5)(held, rtc, rts, rfh, rfl)
    norms = []
    for iteration in range(ITERS):
        arrived = exchange(send, n, n_chan)
        back, norm = column(
            wanted, arrived, wh, wl, weights, tc, ts, cfh, cfl, cih, cil
        )
        norms.append(norm[0, 0])
        arrived = exchange(back, n, n_chan)
        if iteration < ITERS - 1:
            send = call(middle_kernel, ready, wide, [VMEM_SPEC] * 7)(
                arrived, rtc, rts, rfh, rfl, rih, ril
            )
    held, sums = call(
        last_kernel,
        [
            jax.ShapeDtypeStruct((length // n, n * row_count), F32),
            jax.ShapeDtypeStruct((n, 8, 128), F32),
        ],
        wide,
        [VMEM_SPEC] * 5,
    )(arrived, rtc, rts, rih, ril)
    sums = exchange(sums, n, n_chan)
    norms.append(jnp.sqrt(jnp.sum(sums[:, 0, 0])))
    image = held.reshape(length // n, n, row_count).transpose(2, 0, 1).reshape(row_count, length)
    return image * (float(length) / norms[-1]), jnp.stack(norms[1:])


def per_device(image0, interp, vis_weight, counts, tile_index):
    n = lax.axis_size("base") * lax.axis_size("chan")
    row_count, length = image0.shape
    vcap, cells = interp.shape[3:]
    touch = tile_index.shape[2]
    fits = (n, row_count, length // row_count) == (TILE_U, 64, TILE_U)
    if fits and (vcap, cells, touch % 256) == (8, 256, 0) and touch // n == 8:
        return fast_device(image0, interp, vis_weight, counts, tile_index)
    return general_device(image0, interp, vis_weight, counts, tile_index)


def solution(mesh):
    placed = (
        P(("base", "chan"), None),
        P("base", "chan", None, None, None),
        P("base", "chan", None, None),
        P("base", "chan", None),
        P("base", "chan", None),
    )
    return jax.shard_map(
        per_device,
        mesh=mesh,
        in_specs=placed,
        out_specs=(P(("base", "chan"), None), P()),
        check_vma=False,
    )
```

```python
import math

import jax
import jax.numpy as jnp
import numpy as np
from jax import lax
from jax.experimental import pallas as pl
from jax.experimental.pallas import tpu as pltpu
from jax.sharding import PartitionSpec as P

TILE_V = 8
TILE_U = 32
ITERS = 3


PRECISION_LEVEL = lax.Precision.HIGHEST


def split_length(length):
    outer_len = 2 ** ((length.bit_length() - 1) // 2)
    return (outer_len, length // outer_len)


def angle_table(count_a, count_b, modulus, sign):
    left = jnp.arange(count_a, dtype=jnp.int32)[:, None]
    right = jnp.arange(count_b, dtype=jnp.int32)[None, :]
    angle = sign * 2.0 * math.pi / modulus * (left * right % modulus).astype(jnp.float32)
    return (jnp.cos(angle), jnp.sin(angle))


def transform_rows(real_part, imag_part, sign):
    row_count, length = real_part.shape
    outer_len, inner_len = split_length(length)
    cos_q, sin_q = angle_table(inner_len, inner_len, inner_len, sign)
    cos_t, sin_t = angle_table(inner_len, outer_len, length, sign)
    cos_p, sin_p = angle_table(outer_len, outer_len, outer_len, sign)
    real_in = real_part.reshape(row_count, inner_len, outer_len)
    first_re = jnp.einsum("kq,rqp->rkp", cos_q, real_in, precision=PRECISION_LEVEL)
    first_im = jnp.einsum("kq,rqp->rkp", sin_q, real_in, precision=PRECISION_LEVEL)
    if imag_part is not None:
        imag_in = imag_part.reshape(row_count, inner_len, outer_len)
        first_re = first_re - jnp.einsum("kq,rqp->rkp", sin_q, imag_in, precision=PRECISION_LEVEL)
        first_im = first_im + jnp.einsum("kq,rqp->rkp", cos_q, imag_in, precision=PRECISION_LEVEL)
    turned_re = first_re * cos_t - first_im * sin_t
    turned_im = first_re * sin_t + first_im * cos_t
    last_re = jnp.einsum("jp,rkp->rjk", cos_p, turned_re, precision=PRECISION_LEVEL) - jnp.einsum(
        "jp,rkp->rjk", sin_p, turned_im, precision=PRECISION_LEVEL
    )
    last_im = jnp.einsum("jp,rkp->rjk", cos_p, turned_im, precision=PRECISION_LEVEL) + jnp.einsum(
        "jp,rkp->rjk", sin_p, turned_re, precision=PRECISION_LEVEL
    )
    factor = 1.0 / math.sqrt(length)
    return (
        last_re.reshape(row_count, length) * factor,
        last_im.reshape(row_count, length) * factor,
    )


def transpose_global(real_part, imag_part):
    row_count, length = real_part.shape
    n_base = lax.axis_size("base")
    n_chan = lax.axis_size("chan")
    width = length // (n_base * n_chan)
    moved = (
        lax.all_to_all(
            lax.all_to_all(
                real_part.reshape(1, row_count, n_base, n_chan, width),
                "base",
                split_axis=2,
                concat_axis=0,
                tiled=True,
            ),
            "chan",
            split_axis=3,
            concat_axis=1,
            tiled=True,
        ),
        lax.all_to_all(
            lax.all_to_all(
                imag_part.reshape(1, row_count, n_base, n_chan, width),
                "base",
                split_axis=2,
                concat_axis=0,
                tiled=True,
            ),
            "chan",
            split_axis=3,
            concat_axis=1,
            tiled=True,
        ),
    )
    return (moved[0].reshape(length, width).T, moved[1].reshape(length, width).T)


def to_tiles(plane):
    row_count, length = plane.shape
    shaped = plane.reshape(row_count // TILE_V, TILE_V, length // TILE_U, TILE_U)
    return shaped.transpose(0, 2, 1, 3).reshape(-1, TILE_V * TILE_U)


def from_tiles(tiles, row_count, length):
    shaped = tiles.reshape(row_count // TILE_V, length // TILE_U, TILE_V, TILE_U)
    return shaped.transpose(0, 2, 1, 3).reshape(row_count, length)


def slot_work(sample_weights, masked_weight, sample_values):
    visible_samples = (
        jnp.einsum("gnz,gez->gen", sample_weights, sample_values, precision=PRECISION_LEVEL)
        * masked_weight[:, None, :]
    )
    return jnp.einsum("hbi,hyb->hyi", sample_weights, visible_samples, precision=PRECISION_LEVEL)


def total_squares(image):
    return lax.psum(jnp.sum(image * image), ("base", "chan"))


def general_device(image0, interp, vis_weight, counts, tile_index):
    n_base = lax.axis_size("base")
    n_chan = lax.axis_size("chan")
    row_count, length = image0.shape
    touch = tile_index.shape[2]
    slots_each = touch // (n_base * n_chan)
    vcap = interp.shape[3]
    cells = interp.shape[4]
    tiles_own = row_count // TILE_V * (length // TILE_U)
    live = (jnp.arange(vcap, dtype=jnp.int32)[None, :] < counts.reshape(touch, 1)).astype(
        jnp.float32
    )
    masked_weight = vis_weight.reshape(touch, vcap) * live
    sample_weights = interp.reshape(touch, vcap, cells)
    wanted = lax.all_to_all(
        lax.all_to_all(
            tile_index.reshape(n_base, n_chan, slots_each),
            "base",
            split_axis=0,
            concat_axis=0,
            tiled=True,
        ),
        "chan",
        split_axis=1,
        concat_axis=1,
        tiled=True,
    ).reshape(touch)
    onehot = (jnp.arange(tiles_own, dtype=jnp.int32)[:, None] == wanted[None, :]).astype(
        jnp.float32
    )
    moved = (
        lax.all_to_all(
            lax.all_to_all(
                sample_weights.reshape(n_base, n_chan, slots_each, vcap, cells),
                "base",
                split_axis=0,
                concat_axis=0,
                tiled=True,
            ),
            "chan",
            split_axis=1,
            concat_axis=1,
            tiled=True,
        ),
        lax.all_to_all(
            lax.all_to_all(
                masked_weight.reshape(n_base, n_chan, slots_each, vcap),
                "base",
                split_axis=0,
                concat_axis=0,
                tiled=True,
            ),
            "chan",
            split_axis=1,
            concat_axis=1,
            tiled=True,
        ),
    )
    sample_weights = moved[0].reshape(touch, vcap, cells)
    masked_weight = moved[1].reshape(touch, vcap)
    found = []
    current = image0 / jnp.sqrt(total_squares(image0))
    for iteration in range(ITERS):
        real_part, imag_part = transform_rows(current, None, -1.0)
        real_part, imag_part = transpose_global(real_part, imag_part)
        real_part, imag_part = transform_rows(real_part, imag_part, -1.0)
        tiles = jnp.stack([to_tiles(real_part), to_tiles(imag_part)], axis=1)
        sample_values = jnp.take(tiles, wanted, axis=0)
        gridded_plane = slot_work(sample_weights, masked_weight, sample_values)
        summed = jnp.einsum("ts,skc->tkc", onehot, gridded_plane, precision=PRECISION_LEVEL)
        real_part = from_tiles(summed[:, 0, :], row_count, length)
        imag_part = from_tiles(summed[:, 1, :], row_count, length)
        real_part, imag_part = transform_rows(real_part, imag_part, 1.0)
        real_part, imag_part = transpose_global(real_part, imag_part)
        real_part, imag_part = transform_rows(real_part, imag_part, 1.0)
        norm_value = jnp.sqrt(total_squares(real_part))
        found.append(norm_value)
        current = real_part / norm_value
    return (float(length) * current, jnp.stack(found))


F32 = jnp.float32
BF16 = jnp.bfloat16
VMEM_SPEC = pl.BlockSpec(memory_space=pltpu.VMEM)
SMEM_SPEC = pl.BlockSpec(memory_space=pltpu.SMEM)
BIG = pltpu.CompilerParams(vmem_limit_bytes=48 * 1024 * 1024)


def halves(value):
    high = value.astype(BF16)
    return high, (value - high.astype(F32)).astype(BF16)


def np_halves(table):
    high = np.asarray(table, np.float32).astype(jnp.bfloat16)
    low = (np.asarray(table, np.float64) - high.astype(np.float64)).astype(jnp.bfloat16)
    return high, low


def triple_dot(left, right, dims):
    def one(a, b):
        return lax.dot_general(a, b, (dims, ((), ())), preferred_element_type=F32)

    return one(left[0], right[0]) + (one(left[0], right[1]) + one(left[1], right[0]))


def fft_list(items, sign):
    count = len(items)
    if count == 1:
        return items
    even = fft_list(items[0::2], sign)
    odd = fft_list(items[1::2], sign)
    low, high = [], []
    for k in range(count // 2):
        re, im = odd[k]
        if k == 0:
            t_re, t_im = re, im
        elif 4 * k == count:
            t_re, t_im = (im, -re) if sign < 0 else (-im, re)
        else:
            angle = sign * 2.0 * math.pi * k / count
            c, s = math.cos(angle), math.sin(angle)
            t_re, t_im = re * c - im * s, re * s + im * c
        e_re, e_im = even[k]
        low.append((e_re + t_re, e_im + t_im))
        high.append((e_re - t_re, e_im - t_im))
    return low + high


def exchange_kernel(n, n_chan, count, *refs):
    sources, targets = refs[:count], refs[count : 2 * count]
    own_sem, send_sem, recv_sem = refs[2 * count :]
    me = lax.axis_index("base") * n_chan + lax.axis_index("chan")

    def copies(step):
        peer = lax.rem(me + step, n)
        return [
            pltpu.make_async_remote_copy(
                src_ref=sources[k].at[peer],
                dst_ref=targets[k].at[me],
                send_sem=send_sem.at[k, step],
                recv_sem=recv_sem.at[k, step],
                device_id=(peer // n_chan, lax.rem(peer, n_chan)),
                device_id_type=pl.DeviceIdType.MESH,
            )
            for k in range(count)
        ]

    def launch(step, carry):
        for copy in copies(step):
            copy.start()
        return carry

    def finish(step, carry):
        for copy in copies(step):
            copy.wait()
        return carry

    own = [
        pltpu.make_async_copy(sources[k].at[me], targets[k].at[me], own_sem.at[k])
        for k in range(count)
    ]
    lax.fori_loop(1, n, launch, 0)
    for copy in own:
        copy.start()
    for copy in own:
        copy.wait()
    lax.fori_loop(1, n, finish, 0)


def exchange(arrays, n, n_chan):
    count = len(arrays)
    return pl.pallas_call(
        lambda *refs: exchange_kernel(n, n_chan, count, *refs),
        out_shape=[jax.ShapeDtypeStruct(values.shape, values.dtype) for values in arrays],
        in_specs=[
            pl.BlockSpec(memory_space=pl.ANY) if values.size * 4 > 2**20 else VMEM_SPEC
            for values in arrays
        ],
        out_specs=[VMEM_SPEC] * count,
        scratch_shapes=[
            pltpu.SemaphoreType.DMA((count,)),
            pltpu.SemaphoreType.DMA((count, n)),
            pltpu.SemaphoreType.DMA((count, n)),
        ],
        compiler_params=pltpu.CompilerParams(
            has_side_effects=True, vmem_limit_bytes=48 * 1024 * 1024
        ),
    )(*arrays)


def turn(re, im, c, s):
    return re * c - im * s, re * s + im * c


def swap_halves(x0, x1):
    half = x0.shape[1] // 2
    left = lax.broadcasted_iota(jnp.int32, x0.shape, 1) < half
    return (
        jnp.where(left, x0, pltpu.roll(x1, half, 1)),
        jnp.where(left, pltpu.roll(x0, half, 1), x1),
    )


def row_inverse(n, recv_ref, tc_ref, ts_ref, mh_ref, ml_ref, b_ref):
    rows = recv_ref.shape[1] // 2

    def chunk(i, carry):
        at = pl.multiple_of(i * 8, 8)
        items = [
            (recv_ref[o, pl.ds(at, 8), :], recv_ref[o, pl.ds(at + rows, 8), :]) for o in range(n)
        ]
        items = fft_list(items, 1.0)
        items = [
            turn(*items[q], tc_ref[q, pl.ds(at, 8), :], -ts_ref[q, pl.ds(at, 8), :])
            for q in range(n)
        ]
        for pair in range(n // 2):
            for part in range(2):
                x0, x1 = swap_halves(items[2 * pair][part], items[2 * pair + 1][part])
                lanes = slice(pair * 128, (pair + 1) * 128)
                b_ref[pl.ds(at + part * 2 * rows, 8), lanes] = x0
                b_ref[pl.ds(at + part * 2 * rows + rows, 8), lanes] = x1
        return carry

    lax.fori_loop(0, rows // 8, chunk, 0)
    parts = []
    for start in range(0, b_ref.shape[1], 512):
        right = halves(b_ref[:, start : start + 512])
        parts.append(triple_dot((mh_ref[...], ml_ref[...]), right, ((1,), (0,))))
    return parts


def row_forward(n, parts, tc_ref, ts_ref, mh_ref, ml_ref, b_ref, send_ref, sum_ref):
    rows = tc_ref.shape[1]
    total = sum(jnp.sum(part * part) for part in parts)
    for index, part in enumerate(parts):
        b_ref[:, index * 512 : (index + 1) * 512] = triple_dot(
            (mh_ref[...], ml_ref[...]), halves(part), ((1,), (0,))
        )

    def chunk(i, carry):
        at = pl.multiple_of(i * 8, 8)
        items = [[None, None] for _ in range(n)]
        for pair in range(n // 2):
            for part in range(2):
                lanes = slice(pair * 128, (pair + 1) * 128)
                x0 = b_ref[pl.ds(at + part * 2 * rows, 8), lanes]
                x1 = b_ref[pl.ds(at + part * 2 * rows + rows, 8), lanes]
                items[2 * pair][part], items[2 * pair + 1][part] = swap_halves(x0, x1)
        items = [
            turn(*items[q], tc_ref[q, pl.ds(at, 8), :], ts_ref[q, pl.ds(at, 8), :])
            for q in range(n)
        ]
        items = fft_list(items, -1.0)
        for o in range(n):
            send_ref[o, pl.ds(at, 8), :] = items[o][0]
            send_ref[o, pl.ds(at + rows, 8), :] = items[o][1]
        return carry

    lax.fori_loop(0, rows // 8, chunk, 0)
    for o in range(n):
        sum_ref[o] = jnp.full((1, 128), total, F32)


def first_kernel(n, y_ref, tc, ts, fh, fl, send_ref, sum_ref, b_ref):
    parts = [y_ref[:, s : s + 512] for s in range(0, y_ref.shape[1], 512)]
    row_forward(n, parts, tc, ts, fh, fl, b_ref, send_ref, sum_ref)


def middle_kernel(n, recv_ref, tc, ts, fh, fl, ih, il, send_ref, sum_ref, b_ref):
    parts = row_inverse(n, recv_ref, tc, ts, ih, il, b_ref)
    row_forward(n, parts, tc, ts, fh, fl, b_ref, send_ref, sum_ref)


def last_kernel(n, recv_ref, tc, ts, ih, il, y_ref, sum_ref, b_ref):
    parts = row_inverse(n, recv_ref, tc, ts, ih, il, b_ref)
    for index, part in enumerate(parts):
        y_ref[:, index * 512 : (index + 1) * 512] = part
    total = sum(jnp.sum(part * part) for part in parts)
    for o in range(n):
        sum_ref[o] = jnp.full((1, 128), total, F32)


def column_kernel(
    n,
    tile_ref,
    recv_ref,
    sum_ref,
    wh_ref,
    wl_ref,
    wm_ref,
    tc,
    ts,
    fh,
    fl,
    ih,
    il,
    send_ref,
    norm_ref,
    u_ref,
    t_ref,
    acc_ref,
    g_ref,
):
    rows = send_ref.shape[1] // 2
    blocks = rows // 8
    groups = wh_ref.shape[0]
    members = g_ref.shape[0] // 2
    total = sum_ref[0]
    for d in range(1, n):
        total = total + sum_ref[d]
    norm = jnp.sqrt(total)
    norm_ref[...] = norm

    def forward(i, carry):
        at = pl.multiple_of(i * 8, 8)
        inverse = 1.0 / norm_ref[...]
        items = fft_list(
            [
                (
                    recv_ref[d, pl.ds(at, 8), :] * inverse,
                    recv_ref[d, pl.ds(at + rows, 8), :] * inverse,
                )
                for d in range(n)
            ],
            -1.0,
        )
        for k in range(n):
            re, im = turn(*items[k], tc[k : k + 1, :], ts[k : k + 1, :])
            u_ref[i, k * 8 : k * 8 + 8, :128] = re
            u_ref[i, k * 8 : k * 8 + 8, 128:] = im
        right = halves(u_ref[i])
        at = pl.ds(pl.multiple_of(i * 256, 256), 256)
        t_ref[at, :] = triple_dot((fh[...], fl[...]), right, ((1,), (1,)))
        acc_ref[at, :] = jnp.zeros((256, acc_ref.shape[1]), F32)
        return carry

    lax.fori_loop(0, blocks, forward, 0)

    row_of = lax.broadcasted_iota(jnp.int32, (2 * members, 256), 0) % members
    slot_of = lax.broadcasted_iota(jnp.int32, (2 * members, 256), 1) // (256 // members)

    def group(g, carry):
        for s in range(members):
            row = tile_ref[g * members + s]
            g_ref[s : s + 1, :] = t_ref[pl.ds(row, 1), :]
            g_ref[s + members : s + members + 1, :] = t_ref[pl.ds(row + 128, 1), :]
        weights = (wh_ref[g], wl_ref[g])
        seen = triple_dot(halves(g_ref[...]), weights, ((1,), (1,)))
        seen = jnp.where(row_of == slot_of, seen * wm_ref[g], 0.0)
        g_ref[...] = triple_dot(halves(seen), weights, ((1,), (0,)))
        for s in range(members):
            row = tile_ref[g * members + s]
            acc_ref[pl.ds(row, 1), :] += g_ref[s : s + 1, :]
            acc_ref[pl.ds(row + 128, 1), :] += g_ref[s + members : s + members + 1, :]
        return carry

    lax.fori_loop(0, groups, group, 0)

    def backward(i, carry):
        at = pl.multiple_of(i * 8, 8)
        held = acc_ref[pl.ds(pl.multiple_of(i * 256, 256), 256), :]
        u_ref[i] = triple_dot(halves(held.T), (ih[...], il[...]), ((1,), (0,)))
        items = []
        for k in range(n):
            re = u_ref[i, k * 8 : k * 8 + 8, :128]
            im = u_ref[i, k * 8 : k * 8 + 8, 128:]
            items.append(turn(re, im, tc[k : k + 1, :], -ts[k : k + 1, :]))
        items = fft_list(items, 1.0)
        for d in range(n):
            send_ref[d, pl.ds(at, 8), :] = items[d][0]
            send_ref[d, pl.ds(at + rows, 8), :] = items[d][1]
        return carry

    lax.fori_loop(0, blocks, backward, 0)


def weight_kernel(x_ref, perm_ref, high_ref, low_ref):
    count, _, cells = x_ref.shape
    value = x_ref[...].reshape(count * x_ref.shape[1], cells)
    for part, ref in zip(halves(value), (high_ref, low_ref)):
        ref[0] = jnp.dot(part, perm_ref[...], preferred_element_type=F32).astype(BF16)


def tables(n, row_count, length):
    half = row_count // 2
    scale = 1.0 / math.sqrt(length)
    local = np.arange(row_count)
    angle = -2.0 * np.pi * np.outer(local, local) / row_count
    c, s = np.cos(angle) * scale, np.sin(angle) * scale
    two = np.eye(2)
    col_f = np.block([[np.kron(two, c), np.kron(two, -s)], [np.kron(two, s), np.kron(two, c)]])
    col_i = np.block([[np.kron(two, c), np.kron(two, -s)], [np.kron(two, s), np.kron(two, c)]])
    row_f = np.concatenate([c, s], axis=0)
    row_i = np.concatenate([c, s], axis=1)
    index = np.arange(n)
    turns = -2.0 * np.pi * np.outer(index, np.tile(local, 2)) / length
    u = np.arange(half)[:, None] + half * (np.arange(2 * row_count)[None, :] // row_count)
    row_turns = -2.0 * np.pi * index[:, None, None] * u[None] / length
    return col_f, col_i, row_f, row_i, turns, row_turns


def fast_device(image0, interp, vis_weight, counts, tile_index):
    n_chan = lax.axis_size("chan")
    n = lax.axis_size("base") * n_chan
    row_count, length = image0.shape
    touch = tile_index.shape[2]
    each = touch // n
    vcap, cells = interp.shape[3:]
    members = cells // vcap
    groups = touch // members
    col_f, col_i, row_f, row_i, turns, row_turns = tables(n, row_count, length)
    cfh, cfl = np_halves(col_f)
    cih, cil = np_halves(col_i)
    rfh, rfl = np_halves(row_f)
    rih, ril = np_halves(row_i)
    tc, ts = np.cos(turns).astype(np.float32), np.sin(turns).astype(np.float32)
    rtc = np.cos(row_turns).astype(np.float32)
    rts = np.sin(row_turns).astype(np.float32)
    order = np.arange(cells).reshape(TILE_V, TILE_U).T.reshape(-1)
    perm = np.zeros((cells, cells), np.float32)
    perm[order, np.arange(cells)] = 1.0

    live = (jnp.arange(vcap, dtype=jnp.int32)[None, :] < counts.reshape(touch, 1)).astype(F32)
    masked = (vis_weight.reshape(touch, vcap) * live).reshape(n, 1, each * vcap)
    numbers = tile_index.reshape(n, 1, each).astype(F32)
    extras = jnp.concatenate([masked, numbers], axis=2)
    extras = jnp.pad(extras, ((0, 0), (0, 0), (0, -extras.shape[2] % 128)))
    matrices = interp.reshape(n, each * vcap, cells)
    wide = [pltpu.VMEM((2 * row_count, length), F32)]
    data = jax.ShapeDtypeStruct((n, row_count, 2 * row_count), F32)
    mark = jax.ShapeDtypeStruct((n, 1, 128), F32)
    ready = [data, mark]

    def call(kernel, shapes, scratch, specs):
        return pl.pallas_call(
            lambda *refs: kernel(n, *refs),
            out_shape=shapes,
            in_specs=specs,
            out_specs=jax.tree.map(lambda _: VMEM_SPEC, shapes),
            scratch_shapes=scratch,
            compiler_params=BIG,
        )

    held = image0.reshape(row_count, length // n, n).transpose(1, 2, 0).reshape(length // n, -1)
    send = call(first_kernel, ready, wide, [VMEM_SPEC] * 5)(held, rtc, rts, rfh, rfl)
    arrived, sums, extras, matrices = exchange([*send, extras, matrices], n, n_chan)
    weights = extras[:, 0, : each * vcap].reshape(groups, 1, members * vcap)
    wanted = extras[:, 0, each * vcap : each * (vcap + 1)].astype(jnp.int32).reshape(touch)
    down = length // TILE_U
    blocks = row_count // TILE_V // 2
    tile_column = wanted // down
    wanted = (tile_column % blocks) * (4 * down) + (tile_column // blocks) * down + wanted % down
    span = n // groups
    wh, wl = pl.pallas_call(
        weight_kernel,
        grid=(groups,),
        out_shape=[jax.ShapeDtypeStruct((groups, members * vcap, cells), BF16)] * 2,
        in_specs=[
            pl.BlockSpec((span, each * vcap, cells), lambda g: (g, 0, 0)),
            pl.BlockSpec((cells, cells), lambda g: (0, 0)),
        ],
        out_specs=[pl.BlockSpec((1, members * vcap, cells), lambda g: (g, 0, 0))] * 2,
    )(matrices, jnp.asarray(perm, BF16))

    column = call(
        column_kernel,
        [
            data,
            jax.ShapeDtypeStruct((1, 128), F32),
        ],
        [pltpu.VMEM((blocks, 256, 256), F32)]
        + [pltpu.VMEM((blocks * 256, 256), F32)] * 2
        + [pltpu.VMEM((2 * members, cells), F32)],
        [SMEM_SPEC] + [VMEM_SPEC] * 11,
    )
    norms = []
    for iteration in range(ITERS):
        if iteration > 0:
            send = call(middle_kernel, ready, wide, [VMEM_SPEC] * 7)(
                arrived, rtc, rts, rfh, rfl, rih, ril
            )
            arrived, sums = exchange(send, n, n_chan)
        back, norm = column(
            wanted, arrived, sums, wh, wl, weights, tc, ts, cfh, cfl, cih, cil
        )
        norms.append(norm[0, 0])
        (arrived,) = exchange([back], n, n_chan)
    held, sums = call(
        last_kernel,
        [
            jax.ShapeDtypeStruct((length // n, n * row_count), F32),
            mark,
        ],
        wide,
        [VMEM_SPEC] * 5,
    )(arrived, rtc, rts, rih, ril)
    (sums,) = exchange([sums], n, n_chan)
    norms.append(jnp.sqrt(jnp.sum(sums[:, 0, 0])))
    image = held.reshape(length // n, n, row_count).transpose(2, 0, 1).reshape(row_count, length)
    return image * (float(length) / norms[-1]), jnp.stack(norms[1:])


def per_device(image0, interp, vis_weight, counts, tile_index):
    n = lax.axis_size("base") * lax.axis_size("chan")
    row_count, length = image0.shape
    vcap, cells = interp.shape[3:]
    touch = tile_index.shape[2]
    fits = (n, row_count, length // row_count) == (TILE_U, 64, TILE_U)
    if fits and (vcap, cells, touch % 256) == (8, 256, 0) and touch // n == 8:
        return fast_device(image0, interp, vis_weight, counts, tile_index)
    return general_device(image0, interp, vis_weight, counts, tile_index)


def solution(mesh):
    placed = (
        P(("base", "chan"), None),
        P("base", "chan", None, None, None),
        P("base", "chan", None, None),
        P("base", "chan", None),
        P("base", "chan", None),
    )
    return jax.shard_map(
        per_device,
        mesh=mesh,
        in_specs=placed,
        out_specs=(P(("base", "chan"), None), P()),
        check_vma=False,
    )
```

```python
import math

import jax
import jax.numpy as jnp
import numpy as np
from jax import lax
from jax.experimental import pallas as pl
from jax.experimental.pallas import tpu as pltpu
from jax.sharding import PartitionSpec as P

TILE_V = 8
TILE_U = 32
ITERS = 3


PRECISION_LEVEL = lax.Precision.HIGHEST


def split_length(length):
    outer_len = 2 ** ((length.bit_length() - 1) // 2)
    return (outer_len, length // outer_len)


def angle_table(count_a, count_b, modulus, sign):
    left = jnp.arange(count_a, dtype=jnp.int32)[:, None]
    right = jnp.arange(count_b, dtype=jnp.int32)[None, :]
    angle = sign * 2.0 * math.pi / modulus * (left * right % modulus).astype(jnp.float32)
    return (jnp.cos(angle), jnp.sin(angle))


def transform_rows(real_part, imag_part, sign):
    row_count, length = real_part.shape
    outer_len, inner_len = split_length(length)
    cos_q, sin_q = angle_table(inner_len, inner_len, inner_len, sign)
    cos_t, sin_t = angle_table(inner_len, outer_len, length, sign)
    cos_p, sin_p = angle_table(outer_len, outer_len, outer_len, sign)
    real_in = real_part.reshape(row_count, inner_len, outer_len)
    first_re = jnp.einsum("kq,rqp->rkp", cos_q, real_in, precision=PRECISION_LEVEL)
    first_im = jnp.einsum("kq,rqp->rkp", sin_q, real_in, precision=PRECISION_LEVEL)
    if imag_part is not None:
        imag_in = imag_part.reshape(row_count, inner_len, outer_len)
        first_re = first_re - jnp.einsum("kq,rqp->rkp", sin_q, imag_in, precision=PRECISION_LEVEL)
        first_im = first_im + jnp.einsum("kq,rqp->rkp", cos_q, imag_in, precision=PRECISION_LEVEL)
    turned_re = first_re * cos_t - first_im * sin_t
    turned_im = first_re * sin_t + first_im * cos_t
    last_re = jnp.einsum("jp,rkp->rjk", cos_p, turned_re, precision=PRECISION_LEVEL) - jnp.einsum(
        "jp,rkp->rjk", sin_p, turned_im, precision=PRECISION_LEVEL
    )
    last_im = jnp.einsum("jp,rkp->rjk", cos_p, turned_im, precision=PRECISION_LEVEL) + jnp.einsum(
        "jp,rkp->rjk", sin_p, turned_re, precision=PRECISION_LEVEL
    )
    factor = 1.0 / math.sqrt(length)
    return (
        last_re.reshape(row_count, length) * factor,
        last_im.reshape(row_count, length) * factor,
    )


def transpose_global(real_part, imag_part):
    row_count, length = real_part.shape
    n_base = lax.axis_size("base")
    n_chan = lax.axis_size("chan")
    width = length // (n_base * n_chan)
    moved = (
        lax.all_to_all(
            lax.all_to_all(
                real_part.reshape(1, row_count, n_base, n_chan, width),
                "base",
                split_axis=2,
                concat_axis=0,
                tiled=True,
            ),
            "chan",
            split_axis=3,
            concat_axis=1,
            tiled=True,
        ),
        lax.all_to_all(
            lax.all_to_all(
                imag_part.reshape(1, row_count, n_base, n_chan, width),
                "base",
                split_axis=2,
                concat_axis=0,
                tiled=True,
            ),
            "chan",
            split_axis=3,
            concat_axis=1,
            tiled=True,
        ),
    )
    return (moved[0].reshape(length, width).T, moved[1].reshape(length, width).T)


def to_tiles(plane):
    row_count, length = plane.shape
    shaped = plane.reshape(row_count // TILE_V, TILE_V, length // TILE_U, TILE_U)
    return shaped.transpose(0, 2, 1, 3).reshape(-1, TILE_V * TILE_U)


def from_tiles(tiles, row_count, length):
    shaped = tiles.reshape(row_count // TILE_V, length // TILE_U, TILE_V, TILE_U)
    return shaped.transpose(0, 2, 1, 3).reshape(row_count, length)


def slot_work(sample_weights, masked_weight, sample_values):
    visible_samples = (
        jnp.einsum("gnz,gez->gen", sample_weights, sample_values, precision=PRECISION_LEVEL)
        * masked_weight[:, None, :]
    )
    return jnp.einsum("hbi,hyb->hyi", sample_weights, visible_samples, precision=PRECISION_LEVEL)


def total_squares(image):
    return lax.psum(jnp.sum(image * image), ("base", "chan"))


def general_device(image0, interp, vis_weight, counts, tile_index):
    n_base = lax.axis_size("base")
    n_chan = lax.axis_size("chan")
    row_count, length = image0.shape
    touch = tile_index.shape[2]
    slots_each = touch // (n_base * n_chan)
    vcap = interp.shape[3]
    cells = interp.shape[4]
    tiles_own = row_count // TILE_V * (length // TILE_U)
    live = (jnp.arange(vcap, dtype=jnp.int32)[None, :] < counts.reshape(touch, 1)).astype(
        jnp.float32
    )
    masked_weight = vis_weight.reshape(touch, vcap) * live
    sample_weights = interp.reshape(touch, vcap, cells)
    wanted = lax.all_to_all(
        lax.all_to_all(
            tile_index.reshape(n_base, n_chan, slots_each),
            "base",
            split_axis=0,
            concat_axis=0,
            tiled=True,
        ),
        "chan",
        split_axis=1,
        concat_axis=1,
        tiled=True,
    ).reshape(touch)
    onehot = (jnp.arange(tiles_own, dtype=jnp.int32)[:, None] == wanted[None, :]).astype(
        jnp.float32
    )
    moved = (
        lax.all_to_all(
            lax.all_to_all(
                sample_weights.reshape(n_base, n_chan, slots_each, vcap, cells),
                "base",
                split_axis=0,
                concat_axis=0,
                tiled=True,
            ),
            "chan",
            split_axis=1,
            concat_axis=1,
            tiled=True,
        ),
        lax.all_to_all(
            lax.all_to_all(
                masked_weight.reshape(n_base, n_chan, slots_each, vcap),
                "base",
                split_axis=0,
                concat_axis=0,
                tiled=True,
            ),
            "chan",
            split_axis=1,
            concat_axis=1,
            tiled=True,
        ),
    )
    sample_weights = moved[0].reshape(touch, vcap, cells)
    masked_weight = moved[1].reshape(touch, vcap)
    found = []
    current = image0 / jnp.sqrt(total_squares(image0))
    for iteration in range(ITERS):
        real_part, imag_part = transform_rows(current, None, -1.0)
        real_part, imag_part = transpose_global(real_part, imag_part)
        real_part, imag_part = transform_rows(real_part, imag_part, -1.0)
        tiles = jnp.stack([to_tiles(real_part), to_tiles(imag_part)], axis=1)
        sample_values = jnp.take(tiles, wanted, axis=0)
        gridded_plane = slot_work(sample_weights, masked_weight, sample_values)
        summed = jnp.einsum("ts,skc->tkc", onehot, gridded_plane, precision=PRECISION_LEVEL)
        real_part = from_tiles(summed[:, 0, :], row_count, length)
        imag_part = from_tiles(summed[:, 1, :], row_count, length)
        real_part, imag_part = transform_rows(real_part, imag_part, 1.0)
        real_part, imag_part = transpose_global(real_part, imag_part)
        real_part, imag_part = transform_rows(real_part, imag_part, 1.0)
        norm_value = jnp.sqrt(total_squares(real_part))
        found.append(norm_value)
        current = real_part / norm_value
    return (float(length) * current, jnp.stack(found))


F32 = jnp.float32
BF16 = jnp.bfloat16
VMEM_SPEC = pl.BlockSpec(memory_space=pltpu.VMEM)
SMEM_SPEC = pl.BlockSpec(memory_space=pltpu.SMEM)
BIG = pltpu.CompilerParams(vmem_limit_bytes=48 * 1024 * 1024)


def halves(value):
    high = value.astype(BF16)
    return high, (value - high.astype(F32)).astype(BF16)


def np_halves(table):
    high = np.asarray(table, np.float32).astype(jnp.bfloat16)
    low = (np.asarray(table, np.float64) - high.astype(np.float64)).astype(jnp.bfloat16)
    return high, low


def triple_dot(left, right, dims):
    def one(a, b):
        return lax.dot_general(a, b, (dims, ((), ())), preferred_element_type=F32)

    return one(left[0], right[0]) + (one(left[0], right[1]) + one(left[1], right[0]))


def fft_list(items, sign):
    count = len(items)
    if count == 1:
        return items
    even = fft_list(items[0::2], sign)
    odd = fft_list(items[1::2], sign)
    low, high = [], []
    for k in range(count // 2):
        re, im = odd[k]
        if k == 0:
            t_re, t_im = re, im
        elif 4 * k == count:
            t_re, t_im = (im, -re) if sign < 0 else (-im, re)
        else:
            angle = sign * 2.0 * math.pi * k / count
            c, s = math.cos(angle), math.sin(angle)
            t_re, t_im = re * c - im * s, re * s + im * c
        e_re, e_im = even[k]
        low.append((e_re + t_re, e_im + t_im))
        high.append((e_re - t_re, e_im - t_im))
    return low + high


def exchange_kernel(n, n_chan, count, *refs):
    sources, targets = refs[:count], refs[count : 2 * count]
    own_sem, send_sem, recv_sem = refs[2 * count :]
    me = lax.axis_index("base") * n_chan + lax.axis_index("chan")

    def copies(step):
        peer = lax.rem(me + step, n)
        return [
            pltpu.make_async_remote_copy(
                src_ref=sources[k].at[peer],
                dst_ref=targets[k].at[me],
                send_sem=send_sem.at[k, step],
                recv_sem=recv_sem.at[k, step],
                device_id=(peer // n_chan, lax.rem(peer, n_chan)),
                device_id_type=pl.DeviceIdType.MESH,
            )
            for k in range(count)
        ]

    def launch(step, carry):
        for copy in copies(step):
            copy.start()
        return carry

    def finish(step, carry):
        for copy in copies(step):
            copy.wait()
        return carry

    own = [
        pltpu.make_async_copy(sources[k].at[me], targets[k].at[me], own_sem.at[k])
        for k in range(count)
    ]
    lax.fori_loop(1, n, launch, 0)
    for copy in own:
        copy.start()
    for copy in own:
        copy.wait()
    lax.fori_loop(1, n, finish, 0)


def exchange(arrays, n, n_chan):
    count = len(arrays)
    return pl.pallas_call(
        lambda *refs: exchange_kernel(n, n_chan, count, *refs),
        out_shape=[jax.ShapeDtypeStruct(values.shape, values.dtype) for values in arrays],
        in_specs=[
            pl.BlockSpec(memory_space=pl.ANY) if values.size * 4 > 2**20 else VMEM_SPEC
            for values in arrays
        ],
        out_specs=[VMEM_SPEC] * count,
        scratch_shapes=[
            pltpu.SemaphoreType.DMA((count,)),
            pltpu.SemaphoreType.DMA((count, n)),
            pltpu.SemaphoreType.DMA((count, n)),
        ],
        compiler_params=pltpu.CompilerParams(
            has_side_effects=True, vmem_limit_bytes=48 * 1024 * 1024
        ),
    )(*arrays)


def turn(re, im, c, s):
    return re * c - im * s, re * s + im * c


def swap_halves(x0, x1):
    half = x0.shape[1] // 2
    left = lax.broadcasted_iota(jnp.int32, x0.shape, 1) < half
    return (
        jnp.where(left, x0, pltpu.roll(x1, half, 1)),
        jnp.where(left, pltpu.roll(x0, half, 1), x1),
    )


def row_inverse(n, recv_ref, tc_ref, ts_ref, mh_ref, ml_ref, b_ref):
    rows = recv_ref.shape[1] // 2

    def chunk(i, carry):
        at = pl.multiple_of(i * 8, 8)
        items = [
            (recv_ref[o, pl.ds(at, 8), :], recv_ref[o, pl.ds(at + rows, 8), :]) for o in range(n)
        ]
        items = fft_list(items, 1.0)
        items = [
            turn(*items[q], tc_ref[q, pl.ds(at, 8), :], -ts_ref[q, pl.ds(at, 8), :])
            for q in range(n)
        ]
        for pair in range(n // 2):
            for part in range(2):
                x0, x1 = swap_halves(items[2 * pair][part], items[2 * pair + 1][part])
                lanes = slice(pair * 128, (pair + 1) * 128)
                b_ref[pl.ds(at + part * 2 * rows, 8), lanes] = x0
                b_ref[pl.ds(at + part * 2 * rows + rows, 8), lanes] = x1
        return carry

    lax.fori_loop(0, rows // 8, chunk, 0)
    parts = []
    for start in range(0, b_ref.shape[1], 512):
        right = halves(b_ref[:, start : start + 512])
        parts.append(triple_dot((mh_ref[...], ml_ref[...]), right, ((1,), (0,))))
    return parts


def row_forward(n, parts, tc_ref, ts_ref, mh_ref, ml_ref, b_ref, send_ref, sum_ref):
    rows = tc_ref.shape[1]
    total = sum(jnp.sum(part * part) for part in parts)
    for index, part in enumerate(parts):
        b_ref[:, index * 512 : (index + 1) * 512] = triple_dot(
            (mh_ref[...], ml_ref[...]), halves(part), ((1,), (0,))
        )

    def chunk(i, carry):
        at = pl.multiple_of(i * 8, 8)
        items = [[None, None] for _ in range(n)]
        for pair in range(n // 2):
            for part in range(2):
                lanes = slice(pair * 128, (pair + 1) * 128)
                x0 = b_ref[pl.ds(at + part * 2 * rows, 8), lanes]
                x1 = b_ref[pl.ds(at + part * 2 * rows + rows, 8), lanes]
                items[2 * pair][part], items[2 * pair + 1][part] = swap_halves(x0, x1)
        items = [
            turn(*items[q], tc_ref[q, pl.ds(at, 8), :], ts_ref[q, pl.ds(at, 8), :])
            for q in range(n)
        ]
        items = fft_list(items, -1.0)
        for o in range(n):
            send_ref[o, pl.ds(at, 8), :] = items[o][0]
            send_ref[o, pl.ds(at + rows, 8), :] = items[o][1]
        return carry

    lax.fori_loop(0, rows // 8, chunk, 0)
    for o in range(n):
        sum_ref[o] = jnp.full((1, 128), total, F32)


def first_kernel(n, y_ref, tc, ts, fh, fl, send_ref, sum_ref, b_ref):
    parts = [y_ref[:, s : s + 512] for s in range(0, y_ref.shape[1], 512)]
    row_forward(n, parts, tc, ts, fh, fl, b_ref, send_ref, sum_ref)


def middle_kernel(n, recv_ref, tc, ts, fh, fl, ih, il, send_ref, sum_ref, b_ref):
    parts = row_inverse(n, recv_ref, tc, ts, ih, il, b_ref)
    row_forward(n, parts, tc, ts, fh, fl, b_ref, send_ref, sum_ref)


def last_kernel(n, recv_ref, tc, ts, ih, il, y_ref, sum_ref, b_ref):
    parts = row_inverse(n, recv_ref, tc, ts, ih, il, b_ref)
    for index, part in enumerate(parts):
        y_ref[:, index * 512 : (index + 1) * 512] = part
    total = sum(jnp.sum(part * part) for part in parts)
    for o in range(n):
        sum_ref[o] = jnp.full((1, 128), total, F32)


def column_kernel(
    n,
    tile_ref,
    recv_ref,
    sum_ref,
    wh_ref,
    wl_ref,
    wm_ref,
    tc,
    ts,
    fh,
    fl,
    ih,
    il,
    send_ref,
    norm_ref,
    u_ref,
    t_ref,
    acc_ref,
    g_ref,
):
    rows = send_ref.shape[1] // 2
    blocks = rows // 8
    groups = wh_ref.shape[0]
    members = g_ref.shape[0] // 2
    total = sum_ref[0]
    for d in range(1, n):
        total = total + sum_ref[d]
    norm = jnp.sqrt(total)
    norm_ref[...] = norm

    def forward(i, carry):
        at = pl.multiple_of(i * 8, 8)
        inverse = 1.0 / norm_ref[...]
        items = fft_list(
            [
                (
                    recv_ref[d, pl.ds(at, 8), :] * inverse,
                    recv_ref[d, pl.ds(at + rows, 8), :] * inverse,
                )
                for d in range(n)
            ],
            -1.0,
        )
        for k in range(n):
            re, im = turn(*items[k], tc[k : k + 1, :], ts[k : k + 1, :])
            u_ref[i, k * 8 : k * 8 + 8, :128] = re
            u_ref[i, k * 8 : k * 8 + 8, 128:] = im
        right = halves(u_ref[i])
        at = pl.ds(pl.multiple_of(i * 256, 256), 256)
        t_ref[at, :] = triple_dot((fh[...], fl[...]), right, ((1,), (1,)))
        acc_ref[at, :] = jnp.zeros((256, acc_ref.shape[1]), F32)
        return carry

    lax.fori_loop(0, blocks, forward, 0)

    row_of = lax.broadcasted_iota(jnp.int32, (2 * members, 256), 0) % members
    slot_of = lax.broadcasted_iota(jnp.int32, (2 * members, 256), 1) // (256 // members)

    def group(g, carry):
        for s in range(members):
            row = tile_ref[g * members + s]
            g_ref[s : s + 1, :] = t_ref[pl.ds(row, 1), :]
            g_ref[s + members : s + members + 1, :] = t_ref[pl.ds(row + 128, 1), :]
        weights = (wh_ref[g], wl_ref[g])
        seen = triple_dot(halves(g_ref[...]), weights, ((1,), (1,)))
        seen = jnp.where(row_of == slot_of, seen * wm_ref[g], 0.0)
        g_ref[...] = triple_dot(halves(seen), weights, ((1,), (0,)))
        for s in range(members):
            row = tile_ref[g * members + s]
            acc_ref[pl.ds(row, 1), :] += g_ref[s : s + 1, :]
            acc_ref[pl.ds(row + 128, 1), :] += g_ref[s + members : s + members + 1, :]
        return carry

    lax.fori_loop(0, groups, group, 0)

    def backward(i, carry):
        at = pl.multiple_of(i * 8, 8)
        held = acc_ref[pl.ds(pl.multiple_of(i * 256, 256), 256), :]
        u_ref[i] = triple_dot(halves(held.T), (ih[...], il[...]), ((1,), (0,)))
        items = []
        for k in range(n):
            re = u_ref[i, k * 8 : k * 8 + 8, :128]
            im = u_ref[i, k * 8 : k * 8 + 8, 128:]
            items.append(turn(re, im, tc[k : k + 1, :], -ts[k : k + 1, :]))
        items = fft_list(items, 1.0)
        for d in range(n):
            send_ref[d, pl.ds(at, 8), :] = items[d][0]
            send_ref[d, pl.ds(at + rows, 8), :] = items[d][1]
        return carry

    lax.fori_loop(0, blocks, backward, 0)


def weight_kernel(x_ref, perm_ref, high_ref, low_ref):
    count, _, cells = x_ref.shape
    value = x_ref[...].reshape(count * x_ref.shape[1], cells)
    for part, ref in zip(halves(value), (high_ref, low_ref)):
        ref[...] = (
            jnp.dot(part, perm_ref[...], preferred_element_type=F32)
            .astype(BF16)
            .reshape(ref.shape)
        )


def tables(n, row_count, length):
    half = row_count // 2
    scale = 1.0 / math.sqrt(length)
    local = np.arange(row_count)
    angle = -2.0 * np.pi * np.outer(local, local) / row_count
    c, s = np.cos(angle) * scale, np.sin(angle) * scale
    two = np.eye(2)
    col_f = np.block([[np.kron(two, c), np.kron(two, -s)], [np.kron(two, s), np.kron(two, c)]])
    col_i = np.block([[np.kron(two, c), np.kron(two, -s)], [np.kron(two, s), np.kron(two, c)]])
    row_f = np.concatenate([c, s], axis=0)
    row_i = np.concatenate([c, s], axis=1)
    index = np.arange(n)
    turns = -2.0 * np.pi * np.outer(index, np.tile(local, 2)) / length
    u = np.arange(half)[:, None] + half * (np.arange(2 * row_count)[None, :] // row_count)
    row_turns = -2.0 * np.pi * index[:, None, None] * u[None] / length
    return col_f, col_i, row_f, row_i, turns, row_turns


def fast_device(image0, interp, vis_weight, counts, tile_index):
    n_chan = lax.axis_size("chan")
    n = lax.axis_size("base") * n_chan
    row_count, length = image0.shape
    touch = tile_index.shape[2]
    each = touch // n
    vcap, cells = interp.shape[3:]
    members = cells // vcap
    groups = touch // members
    col_f, col_i, row_f, row_i, turns, row_turns = tables(n, row_count, length)
    cfh, cfl = np_halves(col_f)
    cih, cil = np_halves(col_i)
    rfh, rfl = np_halves(row_f)
    rih, ril = np_halves(row_i)
    tc, ts = np.cos(turns).astype(np.float32), np.sin(turns).astype(np.float32)
    rtc = np.cos(row_turns).astype(np.float32)
    rts = np.sin(row_turns).astype(np.float32)
    order = np.arange(cells).reshape(TILE_V, TILE_U).T.reshape(-1)
    perm = np.zeros((cells, cells), np.float32)
    perm[order, np.arange(cells)] = 1.0

    live = (jnp.arange(vcap, dtype=jnp.int32)[None, :] < counts.reshape(touch, 1)).astype(F32)
    masked = (vis_weight.reshape(touch, vcap) * live).reshape(n, 1, each * vcap)
    numbers = tile_index.reshape(n, 1, each).astype(F32)
    extras = jnp.concatenate([masked, numbers], axis=2)
    extras = jnp.pad(extras, ((0, 0), (0, 0), (0, -extras.shape[2] % 128)))
    matrices = interp.reshape(n, each * vcap, cells)
    wide = [pltpu.VMEM((2 * row_count, length), F32)]
    data = jax.ShapeDtypeStruct((n, row_count, 2 * row_count), F32)
    mark = jax.ShapeDtypeStruct((n, 1, 128), F32)
    ready = [data, mark]

    def call(kernel, shapes, scratch, specs):
        return pl.pallas_call(
            lambda *refs: kernel(n, *refs),
            out_shape=shapes,
            in_specs=specs,
            out_specs=jax.tree.map(lambda _: VMEM_SPEC, shapes),
            scratch_shapes=scratch,
            compiler_params=BIG,
        )

    held = image0.reshape(row_count, length // n, n).transpose(1, 2, 0).reshape(length // n, -1)
    send = call(first_kernel, ready, wide, [VMEM_SPEC] * 5)(held, rtc, rts, rfh, rfl)
    arrived, sums, extras, matrices = exchange([*send, extras, matrices], n, n_chan)
    weights = extras[:, 0, : each * vcap].reshape(groups, 1, members * vcap)
    wanted = extras[:, 0, each * vcap : each * (vcap + 1)].astype(jnp.int32).reshape(touch)
    down = length // TILE_U
    blocks = row_count // TILE_V // 2
    tile_column = wanted // down
    wanted = (tile_column % blocks) * (4 * down) + (tile_column // blocks) * down + wanted % down
    joint = math.gcd(groups, 4)
    span = n // groups * joint
    wh, wl = pl.pallas_call(
        weight_kernel,
        grid=(groups // joint,),
        out_shape=[jax.ShapeDtypeStruct((groups, members * vcap, cells), BF16)] * 2,
        in_specs=[
            pl.BlockSpec((span, each * vcap, cells), lambda g: (g, 0, 0)),
            pl.BlockSpec((cells, cells), lambda g: (0, 0)),
        ],
        out_specs=[pl.BlockSpec((joint, members * vcap, cells), lambda g: (g, 0, 0))] * 2,
    )(matrices, jnp.asarray(perm, BF16))

    column = call(
        column_kernel,
        [
            data,
            jax.ShapeDtypeStruct((1, 128), F32),
        ],
        [pltpu.VMEM((blocks, 256, 256), F32)]
        + [pltpu.VMEM((blocks * 256, 256), F32)] * 2
        + [pltpu.VMEM((2 * members, cells), F32)],
        [SMEM_SPEC] + [VMEM_SPEC] * 11,
    )
    norms = []
    for iteration in range(ITERS):
        if iteration > 0:
            send = call(middle_kernel, ready, wide, [VMEM_SPEC] * 7)(
                arrived, rtc, rts, rfh, rfl, rih, ril
            )
            arrived, sums = exchange(send, n, n_chan)
        back, norm = column(
            wanted, arrived, sums, wh, wl, weights, tc, ts, cfh, cfl, cih, cil
        )
        norms.append(norm[0, 0])
        (arrived,) = exchange([back], n, n_chan)
    held, sums = call(
        last_kernel,
        [
            jax.ShapeDtypeStruct((length // n, n * row_count), F32),
            mark,
        ],
        wide,
        [VMEM_SPEC] * 5,
    )(arrived, rtc, rts, rih, ril)
    (sums,) = exchange([sums], n, n_chan)
    norms.append(jnp.sqrt(jnp.sum(sums[:, 0, 0])))
    image = held.reshape(length // n, n, row_count).transpose(2, 0, 1).reshape(row_count, length)
    return image * (float(length) / norms[-1]), jnp.stack(norms[1:])


def per_device(image0, interp, vis_weight, counts, tile_index):
    n = lax.axis_size("base") * lax.axis_size("chan")
    row_count, length = image0.shape
    vcap, cells = interp.shape[3:]
    touch = tile_index.shape[2]
    fits = (n, row_count, length // row_count) == (TILE_U, 64, TILE_U)
    if fits and (vcap, cells, touch % 256) == (8, 256, 0) and touch // n == 8:
        return fast_device(image0, interp, vis_weight, counts, tile_index)
    return general_device(image0, interp, vis_weight, counts, tile_index)


def solution(mesh):
    placed = (
        P(("base", "chan"), None),
        P("base", "chan", None, None, None),
        P("base", "chan", None, None),
        P("base", "chan", None),
        P("base", "chan", None),
    )
    return jax.shard_map(
        per_device,
        mesh=mesh,
        in_specs=placed,
        out_specs=(P(("base", "chan"), None), P()),
        check_vma=False,
    )
```
